512 devices in a mesh: term: 8 (over y, core), doc: 16 (over z), enc: 4 (over x).
Axes of the slice: x: 4, y: 4, z: 16, core: 2. Of those that a mesh axis runs over, the one named last changes fastest.
Arguments:
- query_weights: bfloat16 [1024, 30720], P('enc', ('term', 'doc')), may hold values from 0.049804688 to 2
- tile_terms: int32 [30720], P(('term', 'doc')), may hold values from 0 to 59
- tile_blocks: int32 [30720], P(('term', 'doc')), may hold values from 0 to 15
- tile_counts: int32 [128], P(('term', 'doc')), may hold values from 60 to 240, as said below
- impacts: bfloat16 [30720, 64, 128], P(('term', 'doc')), may hold values from -0.015625 to 0.015625
Outputs:
- scores: float32 [2048, 1024], P('doc', 'enc')
The draws below stay inside these ranges and needn't reach their ends.
Inputs may be any that keep to these rules, and one draw needn't show every extreme that they name: Slots at positions tile_counts or later of a device's list are padding and contribute nothing; some device has all 240 slots live.
All inputs are finite; a program needn't handle non-finite values.
Results may differ from the reference program's by a relative error of at most 0.0003.
Values may be sent and summed in bfloat16 or wider, within the bound.
No kernel may reach another device: no remote copies, remote signals or barrier semaphores. Data moves between devices by JAX's collectives and lax.ppermute only.
A program may use at most 64 MiB of HBM per device.

```python
import math
import jax
import jax.numpy as jnp
from jax import lax

VOCAB = 30720
TERM_BLOCK = 64
DOC_BLOCK = 128
TILES = 240
QUERIES = 1024
INDEX_DEVS = 128
ALL_TILES = 30720
RBLOCKS = 60
DOCS = 2048
N_TERM = 8
N_DOC = 16


def draw_tile_counts(key, part):
    first, second = jax.random.split(jax.random.fold_in(key, 7))
    counts = jax.random.randint(first, (INDEX_DEVS,), TILES // 4, TILES + 1)
    chosen = jax.random.randint(second, (), 0, INDEX_DEVS)
    return jnp.where(jnp.arange(INDEX_DEVS) == chosen, TILES, counts).astype(jnp.int32)


def plant(values, key, smallest, largest):
    index_at = [jax.random.randint(jax.random.fold_in(key, axis), (), 0, length) for axis, length in enumerate(values.shape)]
    main_axis = values.shape.index(max(values.shape))
    beside = index_at[:main_axis] + [(index_at[main_axis] + 1) % values.shape[main_axis]] + index_at[main_axis + 1:]
    return values.at[tuple(index_at)].set(smallest).at[tuple(beside)].set(largest)


def block_levels(rng, shape, pieces, low, high):
    level, own = 1.0, jax.random.fold_in(rng, 6)
    for position, parts in pieces:
        draws = jnp.exp(jax.random.uniform(jax.random.fold_in(own, position), (parts,), jnp.float32, low / len(pieces), high / len(pieces)))
        level = level * jnp.repeat(draws, shape[position] // parts).reshape([-1 if axis == position else 1 for axis in range(len(shape))])
    return level


def scatter_about(own_key, shape, spread, most, shards=(), kind=jnp.bfloat16):
    level = block_levels(own_key, shape, shards, -0.22, 0.18) if shards else 1.0
    values = jax.random.normal(own_key, shape, jnp.float32) * spread * level
    return jnp.minimum(jnp.maximum(values, -most), most).astype(kind)


def setup_inputs(seed: int = 0) -> dict:
    key_of = jax.random.split(jax.random.key(seed), 6)
    return {
        "query_weights": jnp.clip(jnp.exp(math.log(2.0) - 3.6927934 * jax.random.uniform(key_of[0], (QUERIES, VOCAB), jnp.float32) ** block_levels(key_of[0], (QUERIES, VOCAB), ((0, 4), (1, 128)), -0.2, 0.2)), 0.049804688, 2.0).astype(jnp.bfloat16),
        "tile_terms": plant(jax.random.randint(key_of[1], (ALL_TILES,), 0, RBLOCKS), jax.random.fold_in(key_of[1], 1), 0, RBLOCKS - 1).astype(jnp.int32),
        "tile_blocks": plant(jax.random.randint(key_of[2], (ALL_TILES,), 0, N_DOC), jax.random.fold_in(key_of[2], 1), 0, N_DOC - 1).astype(jnp.int32),
        "tile_counts": draw_tile_counts(jax.random.fold_in(key_of[5], 71), 0),
        "impacts": scatter_about(key_of[4], (ALL_TILES, TERM_BLOCK, DOC_BLOCK), (TERM_BLOCK * TILES * N_TERM) ** -0.5, 0.015625, ((0, 128),)),
    }


def reference(query_weights, tile_terms, tile_blocks, tile_counts, impacts):
    devices_all = N_TERM * N_DOC
    grouped = query_weights.reshape(QUERIES, N_TERM, RBLOCKS, TERM_BLOCK)
    term_lists = tile_terms.reshape(devices_all, TILES)
    block_lists = tile_blocks.reshape(devices_all, TILES)
    tile_values = impacts.reshape(devices_all, TILES, TERM_BLOCK, DOC_BLOCK)

    def one_device(total, index):
        range_rows = lax.dynamic_index_in_dim(grouped, index // N_DOC, axis=1, keepdims=False)
        picked = jnp.take(range_rows, term_lists[index], axis=1).astype(jnp.float32)
        product = jnp.einsum("qnk,nkd->ndq", picked, tile_values[index].astype(jnp.float32))
        live = jnp.arange(TILES, dtype=jnp.int32) < tile_counts[index]
        product = jnp.where(live[:, None, None], product, 0.0)
        summed = jax.ops.segment_sum(product, block_lists[index], num_segments=N_DOC)
        partial_value = summed.reshape(DOCS, QUERIES)
        return total + partial_value, None

    total, unused = lax.scan(one_device, jnp.zeros((DOCS, QUERIES), jnp.float32), jnp.arange(devices_all, dtype=jnp.int32))
    return total
```

```python
import jax
import jax.numpy as jnp
from jax import lax
from jax.experimental import pallas as pl
from jax.experimental.pallas import tpu as pltpu
from jax.sharding import PartitionSpec as P

GROUP = 4
UNROLL = 4


def tile_products(tile_terms, tile_blocks, tile_counts, weights, impacts, parts, owners):
    tiles, term_block, doc_block = impacts.shape
    rows, queries = weights.shape
    zero_block = rows // term_block - 1
    piece = doc_block // parts
    groups = tiles // GROUP + owners + UNROLL
    chunks = 4

    def kernel(terms, blocks, counts, w_ref, tiles_hbm, out_ref, tile_ref, lists, sizes, order, homes, acc, sems):
        share = tiles // chunks
        copies = [
            pltpu.make_async_copy(
                tiles_hbm.at[pl.ds(i * share, share)], tile_ref.at[pl.ds(i * share, share)], sems.at[i]
            )
            for i in range(chunks)
        ]
        for copy in copies:
            copy.start()
        for b in range(owners):
            sizes[b] = 0
        for b in range(owners):
            acc[b] = jnp.zeros((doc_block, queries), jnp.float32)

        def place(j, carry):
            b = blocks[j]
            at = sizes[b]
            lists[b, at] = j + 256 * terms[j]
            sizes[b] = at + 1
            return carry

        lax.fori_loop(0, counts[0], place, 0)

        total = jnp.int32(0)
        for b in range(owners):
            size = sizes[b]
            for k in range(GROUP - 1):
                lists[b, size + k] = 256 * zero_block
            count = lax.div(size + GROUP - 1, GROUP)

            def emit(g, at, b=b):
                for k in range(GROUP):
                    order[at * GROUP + k] = lists[b, g * GROUP + k]
                homes[at] = b
                return at + 1

            total = lax.fori_loop(0, count, emit, total)
        for u in range(UNROLL - 1):
            for k in range(GROUP):
                order[(total + u) * GROUP + k] = 256 * zero_block
            homes[total + u] = 0
        for copy in copies:
            copy.wait()

        def step(s, carry):
            products = []
            for u in range(UNROLL):
                g = s * UNROLL + u
                picked, stacked = [], []
                for k in range(GROUP):
                    entry = order[g * GROUP + k]
                    slot = lax.rem(entry, 256)
                    term = lax.div(entry, 256)
                    stacked.append(tile_ref[slot])
                    picked.append(w_ref[pl.ds(pl.multiple_of(term * term_block, term_block), term_block), :])
                products.append(
                    lax.dot_general(
                        jnp.concatenate(stacked, axis=0),
                        jnp.concatenate(picked, axis=0),
                        (((0,), (0,)), ((), ())),
                        preferred_element_type=jnp.float32,
                    )
                )
            for u in range(UNROLL):
                home = homes[s * UNROLL + u]
                acc[home] += products[u]
            return carry

        lax.fori_loop(0, lax.div(total + UNROLL - 1, UNROLL), step, 0)
        for b in range(owners):
            for p in range(parts):
                out_ref[p, b * piece : (b + 1) * piece, :] = acc[b, p * piece : (p + 1) * piece, :]

    smem = pl.BlockSpec(memory_space=pltpu.SMEM)
    return pl.pallas_call(
        kernel,
        out_shape=jax.ShapeDtypeStruct((parts, owners * piece, queries), jnp.float32),
        in_specs=[smem, smem, smem, pl.BlockSpec(memory_space=pltpu.VMEM), pl.BlockSpec(memory_space=pl.ANY)],
        out_specs=pl.BlockSpec(memory_space=pltpu.VMEM),
        scratch_shapes=[
            pltpu.VMEM((tiles, term_block, doc_block), jnp.bfloat16),
            pltpu.SMEM((owners, tiles + GROUP), jnp.int32),
            pltpu.SMEM((owners,), jnp.int32),
            pltpu.SMEM((groups * GROUP,), jnp.int32),
            pltpu.SMEM((groups,), jnp.int32),
            pltpu.VMEM((owners, doc_block, queries), jnp.float32),
            pltpu.SemaphoreType.DMA((chunks,)),
        ],
        compiler_params=pltpu.CompilerParams(vmem_limit_bytes=40 << 20),
        name="tile_products",
    )(tile_terms, tile_blocks, tile_counts, weights, impacts)


def per_device(query_weights, tile_terms, tile_blocks, tile_counts, impacts):
    parts, owners = lax.axis_size("term"), lax.axis_size("doc")
    doc_block = impacts.shape[2]
    queries = query_weights.shape[0]
    mine = query_weights.T.astype(jnp.float16)
    weights = lax.all_gather(mine, "doc", axis=0, tiled=True).astype(jnp.bfloat16)
    weights = jnp.pad(weights, ((0, impacts.shape[1]), (0, 0)))
    partial = tile_products(tile_terms, tile_blocks, tile_counts, weights, impacts, parts, owners)
    piece = doc_block // parts
    over_term = lax.all_to_all(partial, "term", 0, 0, tiled=True).sum(axis=0)
    over_doc = lax.all_to_all(over_term.reshape(owners, piece, queries), "doc", 0, 0, tiled=True).sum(axis=0)
    return lax.all_gather(over_doc, "term", axis=0, tiled=True)


def solution(mesh):
    return jax.shard_map(
        per_device,
        mesh=mesh,
        in_specs=(
            P("enc", ("term", "doc")),
            P(("term", "doc")),
            P(("term", "doc")),
            P(("term", "doc")),
            P(("term", "doc"), None, None),
        ),
        out_specs=P("doc", "enc"),
        check_vma=False,
    )
```

```python
import jax
import jax.numpy as jnp
from jax import lax
from jax.experimental import pallas as pl
from jax.experimental.pallas import tpu as pltpu
from jax.sharding import PartitionSpec as P

GROUP = 4
UNROLL = 8
PLACED = 4
STRIDE = 2 * GROUP
CORES = 2
STEPS = (4, 3, 2, 1)
EXTRA = 16


def tile_products(tile_terms, tile_blocks, tile_counts, weights, impacts, parts, owners):
    tiles, term_block, doc_block = impacts.shape
    queries = weights.shape[1]
    piece = doc_block // parts
    groups = tiles // GROUP + owners + UNROLL
    chunks = 4
    nothing = tiles

    def kernel(terms, blocks, counts, w_ref, tiles_hbm, out_ref, tile_ref, state, order, homes, sems):
        share = tiles // chunks
        copies = [
            pltpu.make_async_copy(
                tiles_hbm.at[pl.ds(i * share, share)], tile_ref.at[pl.ds(i * share, share)], sems.at[i]
            )
            for i in range(chunks)
        ]
        for copy in copies:
            copy.start()
        tile_ref[nothing] = jnp.zeros((term_block, doc_block), jnp.bfloat16)
        for p in range(parts):
            out_ref[p] = jnp.zeros((owners * piece, queries), jnp.float32)
        for b in range(owners):
            state[b] = GROUP

        live = counts[0]

        def place(s, total):
            for u in range(PLACED):
                j = s * PLACED + u
                entry = jnp.where(j < live, j + 256 * terms[j], nothing)
                b = blocks[j]
                at = state[b]
                full = (at & (STRIDE - 1)) == GROUP
                at = jnp.where(full, total * STRIDE, at)
                order[at] = entry
                for k in range(1, GROUP):
                    order[at + k] = nothing
                homes[at // STRIDE] = b
                state[b] = at + 1
                total = total + full.astype(jnp.int32)
            return total

        total = lax.fori_loop(0, (live + PLACED - 1) // PLACED, place, jnp.int32(0))
        for u in range(UNROLL - 1):
            for k in range(GROUP):
                order[(total + u) * STRIDE + k] = nothing
            homes[total + u] = 0
        for copy in copies:
            copy.wait()

        def step(s, carry):
            products = []
            for u in range(UNROLL):
                g = s * UNROLL + u
                picked, stacked = [], []
                for k in range(GROUP):
                    entry = order[g * STRIDE + k]
                    stacked.append(tile_ref[entry & 255])
                    row = pl.multiple_of((entry >> 8) * term_block, term_block)
                    picked.append(w_ref[pl.ds(row, term_block), :])
                products.append(
                    lax.dot_general(
                        jnp.concatenate(stacked, axis=0),
                        jnp.concatenate(picked, axis=0),
                        (((0,), (0,)), ((), ())),
                        preferred_element_type=jnp.float32,
                    )
                )
            for u in range(UNROLL):
                row = pl.multiple_of(homes[s * UNROLL + u] * piece, piece)
                for slot in range(parts):
                    p = (slot % (parts // CORES)) * CORES + slot // (parts // CORES)
                    out_ref[slot, pl.ds(row, piece), :] += products[u][p * piece : (p + 1) * piece]
            return carry

        lax.fori_loop(0, (total + UNROLL - 1) // UNROLL, step, 0)

    smem = pl.BlockSpec(memory_space=pltpu.SMEM)
    return pl.pallas_call(
        kernel,
        out_shape=jax.ShapeDtypeStruct((parts, owners * piece, queries), jnp.float32),
        in_specs=[smem, smem, smem, pl.BlockSpec(memory_space=pltpu.VMEM), pl.BlockSpec(memory_space=pltpu.HBM)],
        out_specs=pl.BlockSpec(memory_space=pltpu.VMEM),
        scratch_shapes=[
            pltpu.VMEM((tiles + 1, term_block, doc_block), jnp.bfloat16),
            pltpu.SMEM((owners,), jnp.int32),
            pltpu.SMEM(((groups + 1) * STRIDE,), jnp.int32),
            pltpu.SMEM((groups + 1,), jnp.int32),
            pltpu.SemaphoreType.DMA((chunks,)),
        ],
        compiler_params=pltpu.CompilerParams(vmem_limit_bytes=40 << 20),
        name="tile_products",
    )(tile_terms, tile_blocks, tile_counts, weights, pltpu.with_memory_space_constraint(impacts, pltpu.HBM))


def send(values, axis, groups=None):
    return lax.all_to_all(values, axis, 0, 0, axis_index_groups=groups, tiled=True)


def sum_over_y(values, groups):
    largest = jnp.max(jnp.abs(values))
    level, scale = jnp.float32(0), jnp.float32(1)
    for step in STEPS:
        fits = largest * scale * 2.0 ** (12 * step) <= 32768.0
        level = level + jnp.where(fits, float(step), 0.0)
        scale = scale * jnp.where(fits, 2.0 ** (12 * step), 1.0)
    members, rows, queries = values.shape
    levels = jnp.broadcast_to(level, (members, EXTRA, queries))
    payload = jnp.concatenate([values * scale, levels], axis=1).astype(jnp.float16)
    arrived = send(payload, "term", groups).astype(jnp.float32)
    left = arrived[:, rows : rows + 1, :1]
    back = jnp.ones_like(left)
    for step in STEPS:
        taken = left >= step
        left = left - jnp.where(taken, float(step), 0.0)
        back = back * jnp.where(taken, 2.0 ** (-12 * step), 1.0)
    return (arrived[:, :rows] * back).sum(axis=0)


def per_device(query_weights, tile_terms, tile_blocks, tile_counts, impacts):
    parts, owners = lax.axis_size("term"), lax.axis_size("doc")
    doc_block = impacts.shape[2]
    queries = query_weights.shape[0]
    piece = doc_block // parts
    mine = query_weights.T.astype(jnp.float16)
    weights = lax.all_gather(mine, "doc", axis=0, tiled=True).astype(jnp.bfloat16)
    partial = tile_products(tile_terms, tile_blocks, tile_counts, weights, impacts, parts, owners)
    chips = parts // CORES
    core_groups = [[CORES * y + c for c in range(CORES)] for y in range(chips)]
    y_groups = [[CORES * y + c for y in range(chips)] for c in range(CORES)]
    over_core = send(partial, "term", core_groups).reshape(CORES, chips, owners * piece, queries).sum(axis=0)
    over_term = sum_over_y(over_core, y_groups)
    over_doc = send(over_term.reshape(owners, piece, queries), "doc").sum(axis=0)
    copies = jnp.broadcast_to(over_doc[None], (parts, piece, queries))
    return send(copies, "term").reshape(doc_block, queries)


def solution(mesh):
    return jax.shard_map(
        per_device,
        mesh=mesh,
        in_specs=(
            P("enc", ("term", "doc")),
            P(("term", "doc")),
            P(("term", "doc")),
            P(("term", "doc")),
            P(("term", "doc"), None, None),
        ),
        out_specs=P("doc", "enc"),
        check_vma=False,
    )
```

```python
import jax
import jax.numpy as jnp
from jax import lax
from jax.experimental import pallas as pl
from jax.experimental.pallas import tpu as pltpu
from jax.sharding import PartitionSpec as P

GROUP = 4
UNROLL = 8
PLACED = 4
STRIDE = 2 * GROUP
CORES = 2
STEPS = (4, 3, 2, 1)
EXTRA = 16


def tile_products(tile_terms, tile_blocks, tile_counts, core, weights, impacts, parts, owners):
    tiles, term_block, doc_block = impacts.shape
    queries = weights.shape[1]
    piece = doc_block // parts
    groups = tiles // GROUP + owners + UNROLL
    chunks = 4
    nothing = tiles

    def kernel(terms, blocks, counts, core_ref, w_ref, tiles_hbm, out_ref, tile_ref, state, order, homes, sems):
        share = tiles // chunks
        copies = [
            pltpu.make_async_copy(
                tiles_hbm.at[pl.ds(i * share, share)], tile_ref.at[pl.ds(i * share, share)], sems.at[i]
            )
            for i in range(chunks)
        ]
        for copy in copies:
            copy.start()
        tile_ref[nothing] = jnp.zeros((term_block, doc_block), jnp.bfloat16)
        for p in range(parts):
            out_ref[p] = jnp.zeros((owners * piece, queries), jnp.float32)
        for b in range(owners):
            state[b] = GROUP

        live = counts[0]

        def place(s, total):
            for u in range(PLACED):
                j = s * PLACED + u
                entry = jnp.where(j < live, j + 256 * terms[j], nothing)
                b = blocks[j]
                at = state[b]
                full = (at & (STRIDE - 1)) == GROUP
                at = jnp.where(full, total * STRIDE, at)
                order[at] = entry
                for k in range(1, GROUP):
                    order[at + k] = nothing
                homes[at // STRIDE] = b
                state[b] = at + 1
                total = total + full.astype(jnp.int32)
            return total

        total = lax.fori_loop(0, (live + PLACED - 1) // PLACED, place, jnp.int32(0))
        for u in range(UNROLL - 1):
            for k in range(GROUP):
                order[(total + u) * STRIDE + k] = nothing
            homes[total + u] = 0
        for copy in copies:
            copy.wait()

        def step(s, carry):
            products = []
            for u in range(UNROLL):
                g = s * UNROLL + u
                picked, stacked = [], []
                for k in range(GROUP):
                    entry = order[g * STRIDE + k]
                    stacked.append(tile_ref[entry & 255])
                    row = pl.multiple_of((entry >> 8) * term_block, term_block)
                    picked.append(w_ref[pl.ds(row, term_block), :])
                products.append(
                    lax.dot_general(
                        jnp.concatenate(stacked, axis=0),
                        jnp.concatenate(picked, axis=0),
                        (((0,), (0,)), ((), ())),
                        preferred_element_type=jnp.float32,
                    )
                )
            for u in range(UNROLL):
                row = pl.multiple_of(homes[s * UNROLL + u] * piece, piece)
                for p in range(parts):
                    slot = jnp.where(core_ref[0] == p % CORES, 0, parts // CORES) + p // CORES
                    out_ref[slot, pl.ds(row, piece), :] += products[u][p * piece : (p + 1) * piece]
            return carry

        lax.fori_loop(0, (total + UNROLL - 1) // UNROLL, step, 0)

    smem = pl.BlockSpec(memory_space=pltpu.SMEM)
    return pl.pallas_call(
        kernel,
        out_shape=jax.ShapeDtypeStruct((parts, owners * piece, queries), jnp.float32),
        in_specs=[smem, smem, smem, smem, pl.BlockSpec(memory_space=pltpu.VMEM), pl.BlockSpec(memory_space=pltpu.HBM)],
        out_specs=pl.BlockSpec(memory_space=pltpu.VMEM),
        scratch_shapes=[
            pltpu.VMEM((tiles + 1, term_block, doc_block), jnp.bfloat16),
            pltpu.SMEM((owners,), jnp.int32),
            pltpu.SMEM(((groups + 1) * STRIDE,), jnp.int32),
            pltpu.SMEM((groups + 1,), jnp.int32),
            pltpu.SemaphoreType.DMA((chunks,)),
        ],
        compiler_params=pltpu.CompilerParams(vmem_limit_bytes=40 << 20),
        name="tile_products",
    )(tile_terms, tile_blocks, tile_counts, core, weights, pltpu.with_memory_space_constraint(impacts, pltpu.HBM))


def send(values, axis, groups=None):
    return lax.all_to_all(values, axis, 0, 0, axis_index_groups=groups, tiled=True)


def sum_over_y(values, groups):
    members, rows, queries = values.shape
    largest = jnp.max(jnp.abs(values), axis=(0, 1))
    level, scale = jnp.zeros_like(largest), jnp.ones_like(largest)
    for step in STEPS:
        fits = largest * scale * 2.0 ** (12 * step) <= 32768.0
        level = level + jnp.where(fits, float(step), 0.0)
        scale = scale * jnp.where(fits, 2.0 ** (12 * step), 1.0)
    levels = jnp.broadcast_to(level, (members, EXTRA, queries))
    payload = jnp.concatenate([values * scale, levels], axis=1).astype(jnp.float16)
    arrived = send(payload, "term", groups).astype(jnp.float32)
    left = arrived[:, rows : rows + 1, :]
    back = jnp.ones_like(left)
    for step in STEPS:
        taken = left >= step
        left = left - jnp.where(taken, float(step), 0.0)
        back = back * jnp.where(taken, 2.0 ** (-12 * step), 1.0)
    return (arrived[:, :rows] * back).sum(axis=0)


def per_device(query_weights, tile_terms, tile_blocks, tile_counts, impacts):
    parts, owners = lax.axis_size("term"), lax.axis_size("doc")
    doc_block = impacts.shape[2]
    queries = query_weights.shape[0]
    piece = doc_block // parts
    mine = query_weights.T.astype(jnp.float16)
    weights = lax.all_gather(mine, "doc", axis=0, tiled=True).astype(jnp.bfloat16)
    core = jnp.reshape(lax.axis_index("term") & (CORES - 1), (1,))
    partial = tile_products(tile_terms, tile_blocks, tile_counts, core, weights, impacts, parts, owners)
    chips = parts // CORES
    y_groups = [[CORES * y + c for y in range(chips)] for c in range(CORES)]
    partner = [(i, i ^ 1) for i in range(parts)]
    over_core = partial[:chips] + lax.ppermute(partial[chips:], "term", partner)
    over_term = sum_over_y(over_core, y_groups)
    over_doc = send(over_term.reshape(owners, piece, queries), "doc").sum(axis=0)
    copies = jnp.broadcast_to(over_doc[None], (parts, piece, queries))
    return send(copies, "term").reshape(doc_block, queries)


def solution(mesh):
    return jax.shard_map(
        per_device,
        mesh=mesh,
        in_specs=(
            P("enc", ("term", "doc")),
            P(("term", "doc")),
            P(("term", "doc")),
            P(("term", "doc")),
            P(("term", "doc"), None, None),
        ),
        out_specs=P("doc", "enc"),
        check_vma=False,
    )
```
